1024 devices in a mesh: dp: 32 (over x_lo, z), seq: 32 (over y, x_hi, core).
Axes of the slice: x: 4 (x_hi: 2, x_lo: 2; x = x_hi * 2 + x_lo), y: 8, z: 16, core: 2. Of those that a mesh axis runs over, the one named last changes fastest.
Arguments:
- tokens: bfloat16 [131072, 8192], P(('dp', 'seq')), may hold values from -6 to 6
- queries: bfloat16 [131072, 1024], P(('dp', 'seq')), may hold values from -110 to 110
- positions: int32 [131072], P(('dp', 'seq')), may hold values from 0 to 1023, as said below
- grad: float32 [8192, 256], P(('dp', 'seq')), may hold values from -6 to 6
- master: float32 [8192, 256], P(('dp', 'seq')), may hold values from -0.0625 to 0.0625
- moment1: float32 [8192, 256], P(('dp', 'seq')), may hold values from -1.8 to 1.8
- moment2: float32 [8192, 256], P(('dp', 'seq')), may hold values from 0.5 to 4
- step: int32 [1], replicated, may hold values from 1 to 8
Outputs:
- attention: bfloat16 [131072, 1024], P(('dp', 'seq'))
- new_master: float32 [8192, 256], P(('dp', 'seq'))
- new_first: float32 [8192, 256], P(('dp', 'seq'))
- new_second: float32 [8192, 256], P(('dp', 'seq'))
The draws below stay inside these ranges and needn't reach their ends.
Inputs may be any that keep to these rules, and one draw needn't show every extreme that they name: `positions`: the sequence is a pack of documents of 1 to 1024 tokens, one of exactly 1024; a position is 0 at the first token of each document and rises by one from token to token inside a document.
All inputs are finite; a program needn't handle non-finite values.
Results may differ from the reference program's by a relative error of at most 0.014.
The reference program's roundings to bfloat16 on the way (of `weight`, `rotated` and `probs`) count: a program that leaves them out, or rounds other values in their place, can miss the bound.
Values may be sent and summed in bfloat16 or wider, within the bound.
No kernel may reach another device: no remote copies, remote signals or barrier semaphores. Data moves between devices by JAX's collectives and lax.ppermute only.
A program may use at most 32 MiB of HBM per device.

```python
import math
import jax
import jax.numpy as jnp
from jax import lax

D = 8192
HD = 128
GROUP = 8
TOK_DEV = 128
DOC_MAX = 1024
SEQLEN = 131072


def draw_queries(key, part):
    shape = (SEQLEN, GROUP * HD)
    key_base = jax.random.fold_in(key, 11)
    values_out = jnp.clip(jax.random.normal(key_base, shape, jnp.float32), -6.0, 6.0)
    return values_out.astype(jnp.bfloat16)


def draw_positions(key, part):
    length_key = jax.random.fold_in(key, 21)
    index = jnp.arange(SEQLEN, dtype=jnp.int32)
    lengths = jax.random.randint(length_key, (SEQLEN,), 1, DOC_MAX + 1).astype(jnp.int32)
    lengths = jnp.where(index == 0, DOC_MAX, lengths).astype(jnp.int32)
    ends = jnp.cumsum(lengths).astype(jnp.int32)
    starts = (ends - lengths).astype(jnp.int32)
    doc_ids = jnp.searchsorted(ends, index, side='right').astype(jnp.int32)
    return (index - starts[doc_ids]).astype(jnp.int32)


def steps_of(own_key, dims, cuts, smallest, largest):
    factor_of, own = 1.0, jax.random.fold_in(own_key, 6)
    for position, blocks in cuts:
        heights = jnp.exp(jax.random.uniform(jax.random.fold_in(own, position), (blocks,), jnp.float32, smallest / len(cuts), largest / len(cuts)))
        factor_of = factor_of * jnp.repeat(heights, dims[position] // blocks).reshape([-1 if axis == position else 1 for axis in range(len(dims))])
    return factor_of


def noise(rng, extent, width, reach, pieces=(), kind=jnp.bfloat16):
    result = jax.random.normal(rng, extent, jnp.float32) * width
    if len(pieces) > 0:
        result = steps_of(rng, extent, pieces, -0.22, 0.18) * result
    return jnp.clip(result, min=-reach, max=reach).astype(kind)


def setup_inputs(seed: int = 0) -> dict:
    arg_keys = jax.random.split(jax.random.key(seed), 9)
    return {
        "tokens": noise(arg_keys[0], (SEQLEN, D), 1.0, 6.0, ((0, 1024),)),
        "queries": draw_queries(jax.random.fold_in(arg_keys[8], 71), 0),
        "positions": draw_positions(jax.random.fold_in(arg_keys[8], 71), 0),
        "grad": noise(arg_keys[3], (D, 2 * HD), 1.0, 6.0, ((0, 1024),), jnp.float32),
        "master": noise(arg_keys[4], (D, 2 * HD), D ** -0.5, 0.0625, ((0, 1024),), jnp.float32),
        "moment1": noise(arg_keys[5], (D, 2 * HD), 0.3, 1.8, ((0, 1024),), jnp.float32),
        "moment2": jnp.clip(jnp.exp(math.log(4.0) - 2.0794415 * jax.random.uniform(arg_keys[6], (D, 2 * HD), jnp.float32) ** steps_of(arg_keys[6], (D, 2 * HD), ((0, 1024),), -0.2, 0.2)), 0.5, 4.0),
        "step": jax.random.randint(arg_keys[7], (1,), 1, 9).astype(jnp.int32),
    }


beta_one = 0.9
beta_two = 0.95
learn_rate = 0.02
adam_eps = 1e-08
rope_base = 500000.0
masked_score = -1e+30

def rotate_pairs(values_in, places):
    half_width = values_in.shape[-1] // 2
    freqs = jnp.exp(jnp.arange(half_width, dtype=jnp.float32) * (-2.0 * math.log(rope_base) / values_in.shape[-1]))
    angles = places.astype(jnp.float32)[:, None, None] * freqs
    cosine = jnp.cos(angles)
    sine = jnp.sin(angles)
    first = values_in[..., :half_width]
    second = values_in[..., half_width:]
    return jnp.concatenate([first * cosine - second * sine, second * cosine + first * sine], axis=-1)

def adam_update(grad, master, moment1, moment2, step):
    counter = step[0].astype(jnp.float32)
    new_first = beta_one * moment1 + (1.0 - beta_one) * grad
    new_second = beta_two * moment2 + (1.0 - beta_two) * grad * grad
    fixed_first = new_first / (1.0 - jnp.power(jnp.float32(beta_one), counter))
    fixed_second = new_second / (1.0 - jnp.power(jnp.float32(beta_two), counter))
    new_master = master - learn_rate * fixed_first / (jnp.sqrt(fixed_second) + adam_eps)
    return (new_master, new_first, new_second)

def attend_rows(query_rows, query_global, query_places, keys, values_v, key_global):
    row_count = query_rows.shape[0]
    block = 512 if row_count % 512 == 0 else row_count

    def one_block(triple):
        rows, index, places = triple
        scores = jnp.dot(rows, keys.T, preferred_element_type=jnp.float32) * rows.shape[-1] ** (-0.5)
        allowed = (key_global[None, :] <= index[:, None]) & (key_global[None, :] >= (index - places)[:, None])
        scores = jnp.where(allowed, scores, masked_score)
        top_score = lax.optimization_barrier(jnp.max(scores, axis=1, keepdims=True))
        weights = jnp.exp(scores - top_score)
        totals = lax.optimization_barrier(jnp.sum(weights, axis=1, keepdims=True))
        probs = (weights / totals).astype(jnp.bfloat16)
        return jnp.dot(probs, values_v, preferred_element_type=jnp.float32).astype(jnp.bfloat16)
    blocks = lax.map(one_block, (query_rows.reshape(-1, block, query_rows.shape[1]), query_global.reshape(-1, block), query_places.reshape(-1, block)))
    return blocks.reshape(row_count, -1)

def reference(tokens, queries, positions, grad, master, moment1, moment2, step):
    new_master, new_first, new_second = adam_update(grad, master, moment1, moment2, step)
    weight = new_master.astype(jnp.bfloat16)
    head_dim = weight.shape[1] // 2
    projected = jnp.dot(tokens, weight, preferred_element_type=jnp.float32)
    keys = rotate_pairs(projected[:, None, :head_dim], positions)[:, 0].astype(jnp.bfloat16)
    values_v = projected[:, head_dim:].astype(jnp.bfloat16)
    rotated = rotate_pairs(queries.astype(jnp.float32).reshape(SEQLEN, GROUP, head_dim), positions).astype(jnp.bfloat16)
    padded_keys = jnp.concatenate([jnp.zeros((DOC_MAX, head_dim), keys.dtype), keys], axis=0)
    padded_values = jnp.concatenate([jnp.zeros((DOC_MAX, head_dim), values_v.dtype), values_v], axis=0)
    local_index = jnp.arange(TOK_DEV, dtype=jnp.int32)
    window_index = jnp.arange(DOC_MAX + TOK_DEV, dtype=jnp.int32)

    def one_block(start):
        rows = lax.dynamic_slice_in_dim(rotated, start, TOK_DEV, 0).reshape(TOK_DEV * GROUP, head_dim)
        places = lax.dynamic_slice_in_dim(positions, start, TOK_DEV, 0)
        query_global = jnp.repeat(start + local_index, GROUP)
        query_places = jnp.repeat(places, GROUP)
        block_keys = lax.dynamic_slice_in_dim(padded_keys, start, DOC_MAX + TOK_DEV, 0)
        block_values = lax.dynamic_slice_in_dim(padded_values, start, DOC_MAX + TOK_DEV, 0)
        key_global = start - DOC_MAX + window_index
        return attend_rows(rows, query_global, query_places, block_keys, block_values, key_global).reshape(TOK_DEV, GROUP * head_dim)
    starts = jnp.arange(SEQLEN // TOK_DEV, dtype=jnp.int32) * TOK_DEV
    attention = lax.map(one_block, starts).reshape(SEQLEN, GROUP * head_dim)
    return (attention, new_master, new_first, new_second)
```

```python
import math

import jax
import jax.numpy as jnp
from jax import lax
from jax.sharding import Mesh
from jax.sharding import PartitionSpec as P

GROUP = 8
CORE = "core"
ALONG_Y = "y"
ALONG_Z = "z"
ALONG_X = ("x_lo", "x_hi")
X_HI = "x_hi"
EVERY = ("x_lo", "z", "y", "x_hi", "core")
CHIPS = ("x_lo", "z", "y", "x_hi")


beta_one = 0.9
beta_two = 0.95
learn_rate = 0.02
adam_eps = 1e-08
rope_base = 500000.0
masked_score = -1e30


def from_everyone(x, axis):
    copies = jnp.broadcast_to(x, (lax.axis_size(axis), *x.shape))
    return lax.all_to_all(copies, axis, split_axis=0, concat_axis=0, tiled=True)


def column_halves(rows, axes):
    half = rows.shape[1] // 2
    for_core = jnp.stack([rows[:, :half], rows[:, half:]])
    reach = lax.axis_size(axes[0])
    copies = jnp.broadcast_to(for_core, (reach, *for_core.shape)).reshape(-1, *for_core.shape[1:])
    return lax.all_to_all(copies, axes, split_axis=0, concat_axis=0, tiled=True)


def other_core(value):
    return lax.ppermute(value, CORE, [(0, 1), (1, 0)])


def shifted(value, axis, steps):
    count = lax.axis_size(axis)
    return lax.ppermute(value, axis, [(source, source + steps) for source in range(count - steps)])


def rotate_pairs(values_in, places):
    half_width = values_in.shape[-1] // 2
    freqs = jnp.exp(
        jnp.arange(half_width, dtype=jnp.float32)
        * (-2.0 * math.log(rope_base) / values_in.shape[-1])
    )
    angles = places.astype(jnp.float32)[:, None, None] * freqs
    cosine = jnp.cos(angles)
    sine = jnp.sin(angles)
    first = values_in[..., :half_width]
    second = values_in[..., half_width:]
    return jnp.concatenate(
        [first * cosine - second * sine, second * cosine + first * sine], axis=-1
    )


def adam_update(grad, master, moment1, moment2, step):
    counter = step[0].astype(jnp.float32)
    new_first = beta_one * moment1 + (1.0 - beta_one) * grad
    new_second = beta_two * moment2 + (1.0 - beta_two) * grad * grad
    fixed_first = new_first / (1.0 - jnp.power(jnp.float32(beta_one), counter))
    fixed_second = new_second / (1.0 - jnp.power(jnp.float32(beta_two), counter))
    new_master = master - learn_rate * fixed_first / (jnp.sqrt(fixed_second) + adam_eps)
    return (new_master, new_first, new_second)


def attend_rows(query_rows, query_global, query_places, keys, values_v, key_global):
    row_count = query_rows.shape[0]
    block = 512

    def one_block(triple):
        rows, index, places = triple
        scores = jnp.einsum(
            "rd,kd->rk", rows, keys, preferred_element_type=jnp.float32
        ) * rows.shape[-1] ** (-0.5)
        allowed = (key_global[None, :] <= index[:, None]) & (
            key_global[None, :] >= (index - places)[:, None]
        )
        scores = jnp.where(allowed, scores, masked_score)
        top_score = jnp.max(scores, axis=1, keepdims=True)
        weights = jnp.exp(scores - top_score)
        totals = jnp.sum(weights, axis=1, keepdims=True)
        probs = (weights / totals).astype(jnp.bfloat16)
        return jnp.dot(probs, values_v, preferred_element_type=jnp.float32).astype(jnp.bfloat16)

    blocks = lax.map(
        one_block,
        (
            query_rows.reshape(-1, block, query_rows.shape[1]),
            query_global.reshape(-1, block),
            query_places.reshape(-1, block),
        ),
    )
    return blocks.reshape(row_count, -1)


def local(tokens, queries, positions, grad, master, moment1, moment2, step):
    core = lax.axis_index(CORE)
    tokens_other = other_core(tokens)
    places_both = lax.all_gather(positions, CORE, axis=0, tiled=True)
    new_master, new_first, new_second = adam_update(grad, master, moment1, moment2, step)
    weight = new_master.astype(jnp.bfloat16)
    head_dim = weight.shape[1] // 2
    local_count = tokens.shape[0]
    chip_count = 2 * local_count
    over_z = column_halves(weight, (ALONG_Z, CORE))
    over_y = from_everyone(over_z.reshape(-1, head_dim), ALONG_Y)
    over_x = from_everyone(over_y.reshape(-1, head_dim), ALONG_X)
    size = lax.axis_size
    pieces = over_x.reshape(
        size("x_lo"), size("x_hi"), size("y"), size("z"), 2 * weight.shape[0], head_dim
    )
    columns = pieces.transpose(0, 3, 2, 1, 4, 5).reshape(-1, head_dim)
    mine = jnp.dot(tokens, columns, preferred_element_type=jnp.float32)
    theirs = jnp.dot(tokens_other, columns, preferred_element_type=jnp.float32)
    first_core = core == 0
    projected = jnp.concatenate(
        [jnp.where(first_core, mine, theirs), jnp.where(first_core, theirs, mine)], axis=0
    )
    turned = rotate_pairs(projected[:, None, :], places_both)[:, 0]
    half_kv = jnp.where(first_core, turned, projected).astype(jnp.bfloat16)
    row_kv = lax.all_gather(half_kv, X_HI, axis=0, tiled=True)
    one_back = shifted(row_kv, CHIPS, 2)
    two_back = shifted(row_kv, CHIPS, 4)
    row_both = lax.all_gather(row_kv, CORE, axis=0)
    back_both = lax.all_gather(jnp.concatenate([two_back, one_back], axis=0), CORE, axis=0)
    window = jnp.concatenate([back_both, row_both], axis=1)
    rotated = rotate_pairs(
        queries.astype(jnp.float32).reshape(local_count, GROUP, head_dim), positions
    ).astype(jnp.bfloat16)
    row_tokens = row_kv.shape[0]
    reach = 2 * row_tokens
    row_index = lax.axis_index(("x_lo", "z", "y"))
    offset = lax.axis_index(("x_hi", "core")) * local_count
    near = lax.dynamic_slice_in_dim(window, offset, reach + local_count, 1)
    window_start = row_index * row_tokens - reach
    key_global = window_start + offset + jnp.arange(reach + local_count, dtype=jnp.int32)
    query_global = jnp.repeat(
        row_index * row_tokens + offset + jnp.arange(local_count, dtype=jnp.int32), GROUP
    )
    query_places = jnp.repeat(positions, GROUP)
    results = attend_rows(
        rotated.reshape(local_count * GROUP, head_dim),
        query_global,
        query_places,
        near[0],
        near[1],
        key_global,
    )
    attention = results.reshape(local_count, GROUP * head_dim)
    return (attention, new_master, new_first, new_second)


def solution(mesh):
    finer = Mesh(mesh.devices.reshape(2, 16, 8, 2, 2), EVERY)
    rows = P(EVERY, None)
    placed = (rows, rows, P(EVERY), rows, rows, rows, rows, P())
    return jax.shard_map(
        local,
        mesh=finer,
        in_specs=placed,
        out_specs=(rows, rows, rows, rows),
        check_vma=False,
    )
```

```python
import math

import jax
import jax.numpy as jnp
from jax import lax
from jax.experimental import pallas as pl
from jax.experimental.pallas import tpu as pltpu
from jax.sharding import Mesh
from jax.sharding import PartitionSpec as P


CORE = "core"
ALONG_Y = "y"
ALONG_Z = "z"
X_HI = "x_hi"
EVERY = ("x_lo", "z", "y", "x_hi", "core")
CHIPS = ("x_lo", "z", "y", "x_hi")


beta_one = 0.9
beta_two = 0.95
learn_rate = 0.02
adam_eps = 1e-08
rope_base = 500000.0
masked_score = -1e30


def adam_update(grad, master, moment1, moment2, step):
    counter = step[0].astype(jnp.float32)
    new_first = beta_one * moment1 + (1.0 - beta_one) * grad
    new_second = beta_two * moment2 + (1.0 - beta_two) * grad * grad
    fixed_first = new_first / (1.0 - jnp.power(jnp.float32(beta_one), counter))
    fixed_second = new_second / (1.0 - jnp.power(jnp.float32(beta_two), counter))
    new_master = master - learn_rate * fixed_first / (jnp.sqrt(fixed_second) + adam_eps)
    return (new_master, new_first, new_second)


def on_chip(count):
    return [pl.BlockSpec(memory_space=pltpu.VMEM)] * count


def room(mib):
    return pltpu.CompilerParams(vmem_limit_bytes=mib * 2**20)


def split_kernel(tokens_ref, out_ref):
    span = 512
    source = lax.broadcasted_iota(jnp.int32, (span, span), 0)
    target = lax.broadcasted_iota(jnp.int32, (span, span), 1)
    goal = (
        (((source >> 3) & 3) << 7)
        | ((source >> 8) << 6)
        | (((source >> 5) & 7) << 3)
        | (source & 7)
    )
    chosen = (goal == target).astype(jnp.float32).astype(jnp.bfloat16)
    count = tokens_ref.shape[0]
    for x_lo in range(2):
        stacked = jnp.concatenate(
            [
                tokens_ref[:, (8 * x_lo + part) * span : (8 * x_lo + part + 1) * span]
                for part in range(8)
            ],
            axis=0,
        )
        moved = jnp.dot(stacked, chosen, preferred_element_type=jnp.float32).astype(jnp.bfloat16)
        for part in range(8):
            for kind in range(4):
                out_ref[4 * x_lo + kind, :, part * 128 : (part + 1) * 128] = moved[
                    part * count : (part + 1) * count, kind * 128 : (kind + 1) * 128
                ]


def split_columns(tokens):
    count, width = tokens.shape
    return pl.pallas_call(
        split_kernel,
        out_shape=jax.ShapeDtypeStruct((8, count, width // 8), tokens.dtype),
        in_specs=on_chip(1),
        out_specs=on_chip(1)[0],
        compiler_params=room(20),
        cost_estimate=pl.CostEstimate(
            flops=2 * count * width * 512, bytes_accessed=4 * count * width, transcendentals=0
        ),
    )(tokens)


def partial_kernel(weight_ref, tokens_ref, out_ref):
    kinds, count, depth = tokens_ref.shape
    head_dim = weight_ref.shape[1] // 2
    part = jnp.dot(
        tokens_ref[...].reshape(kinds * count, depth),
        weight_ref[...],
        preferred_element_type=jnp.float32,
    )
    part = part.reshape(kinds, count, 2 * head_dim)
    keys = part[:, :, :head_dim]
    high = keys.astype(jnp.bfloat16)
    out_ref[:, :, :head_dim] = high
    out_ref[:, :, head_dim : 2 * head_dim] = (keys - high.astype(jnp.float32)).astype(jnp.bfloat16)
    out_ref[:, :, 2 * head_dim :] = part[:, :, head_dim:].astype(jnp.bfloat16)


def partial_products(weight, tokens):
    kinds, count, depth = tokens.shape
    width = weight.shape[1] // 2 * 3
    return pl.pallas_call(
        partial_kernel,
        out_shape=jax.ShapeDtypeStruct((kinds, count, width), jnp.bfloat16),
        in_specs=on_chip(2),
        out_specs=on_chip(1)[0],
        compiler_params=room(20),
        cost_estimate=pl.CostEstimate(
            flops=2 * kinds * count * weight.shape[1] * depth,
            bytes_accessed=2 * kinds * count * (width + depth),
            transcendentals=0,
        ),
    )(weight, tokens)


def turned(values, cosine, sine):
    return values * cosine + pltpu.roll(values, values.shape[1] // 2, 1) * sine


def sum_kernel(parts_ref, cosine_ref, sine_ref, out_ref):
    head_dim = parts_ref.shape[2] // 3
    total = jnp.sum(parts_ref[...].astype(jnp.float32), axis=0)
    keys = total[:, :head_dim] + total[:, head_dim : 2 * head_dim]
    out_ref[:, :head_dim] = turned(keys, cosine_ref[...], sine_ref[...]).astype(jnp.bfloat16)
    out_ref[:, head_dim:] = total[:, 2 * head_dim :].astype(jnp.bfloat16)


def summed(parts, cosine, sine):
    kinds, count, width = parts.shape
    return pl.pallas_call(
        sum_kernel,
        out_shape=jax.ShapeDtypeStruct((count, width // 3 * 2), jnp.bfloat16),
        in_specs=on_chip(3),
        out_specs=on_chip(1)[0],
        compiler_params=room(8),
        cost_estimate=pl.CostEstimate(
            flops=kinds * count * width, bytes_accessed=2 * kinds * count * width, transcendentals=0
        ),
    )(parts, cosine, sine)


def attend_kernel(
    offset_ref, back_ref, row_ref, queries_ref, first_ref, cosine_ref, sine_ref, out_ref, window
):
    count, width = queries_ref.shape
    head_dim = cosine_ref.shape[1]
    held, reach = back_ref.shape[0], window.shape[0] - row_ref.shape[0]
    window[:held] = back_ref[...]
    window[held:] = row_ref[...]
    seen = reach + count
    near = pl.ds(pl.multiple_of(offset_ref[0], 128), seen)
    keys = window[near, :head_dim]
    values = window[near, head_dim:]
    row = lax.broadcasted_iota(jnp.int32, (count, head_dim), 0)
    column = lax.broadcasted_iota(jnp.int32, (count, head_dim), 1)
    first = first_ref[...]
    bias = jnp.concatenate(
        [
            jnp.where(
                (column + (start - reach) <= row) & (column + (start - reach) >= first),
                0.0,
                masked_score,
            )
            for start in range(0, seen, head_dim)
        ],
        axis=1,
    )
    cosine, sine = cosine_ref[...], sine_ref[...]
    scale = head_dim**-0.5 * math.log2(math.e)
    for head in range(width // head_dim):
        lanes = slice(head * head_dim, (head + 1) * head_dim)
        rows = turned(queries_ref[:, lanes].astype(jnp.float32), cosine, sine)
        scores = lax.dot_general(
            rows.astype(jnp.bfloat16),
            keys,
            (((1,), (1,)), ((), ())),
            preferred_element_type=jnp.float32,
        )
        scores = scores + bias
        top_score = jnp.max(scores, axis=1, keepdims=True)
        weights = jnp.exp2((scores - top_score) * scale)
        share = 1.0 / jnp.sum(weights, axis=1, keepdims=True)
        probs = (weights * share).astype(jnp.bfloat16)
        out_ref[:, lanes] = jnp.dot(
            probs, values, preferred_element_type=jnp.float32
        ).astype(jnp.bfloat16)


def attend(offset, back, row, queries, first, cosine, sine):
    count, width = queries.shape
    return pl.pallas_call(
        attend_kernel,
        out_shape=jax.ShapeDtypeStruct((count, width), jnp.bfloat16),
        in_specs=[pl.BlockSpec(memory_space=pltpu.SMEM), *on_chip(6)],
        out_specs=on_chip(1)[0],
        scratch_shapes=[pltpu.VMEM((back.shape[0] + row.shape[0], row.shape[1]), jnp.bfloat16)],
        compiler_params=room(20),
        cost_estimate=pl.CostEstimate(
            flops=4 * count * width * 1152,
            bytes_accessed=4 * count * width + 2 * back.size + 2 * row.size,
            transcendentals=count * width * 9,
        ),
    )(offset, back, row, queries, first, cosine, sine)


def rotation_tables(places, head_dim):
    half_width = head_dim // 2
    freqs = jnp.exp(
        jnp.arange(half_width, dtype=jnp.float32) * (-2.0 * math.log(rope_base) / head_dim)
    )
    angles = places.astype(jnp.float32)[:, None] * freqs
    cosine = jnp.cos(angles)
    sine = jnp.sin(angles)
    return (
        jnp.concatenate([cosine, cosine], axis=1),
        jnp.concatenate([-sine, sine], axis=1),
    )


def shifted(value, axis, steps):
    count = lax.axis_size(axis)
    return lax.ppermute(value, axis, [(source, source + steps) for source in range(count - steps)])


def compute(tokens, queries, positions, grad, master, moment1, moment2, step):
    head_dim = master.shape[1] // 2
    local_count = tokens.shape[0]
    ring = ("x_lo", "x_hi", "core")
    new_master, new_first, new_second = adam_update(grad, master, moment1, moment2, step)
    weight = new_master.astype(jnp.bfloat16)
    over_z = lax.all_gather(weight, ALONG_Z, axis=0, tiled=True)
    sorted_tokens = split_columns(tokens)
    tokens_here = lax.all_to_all(
        sorted_tokens, ring, split_axis=0, concat_axis=0, tiled=True
    )
    cosine, sine = rotation_tables(positions, head_dim)
    first = jnp.broadcast_to(
        (jnp.arange(local_count, dtype=jnp.int32) - positions)[:, None],
        (local_count, head_dim),
    )
    over_y = lax.all_gather(over_z, ALONG_Y, axis=0, tiled=True)
    size = lax.axis_size
    rows_here = over_y.reshape(size(ALONG_Y), size(ALONG_Z), weight.shape[0], 2 * head_dim)
    rows_here = rows_here.transpose(1, 0, 2, 3).reshape(-1, 2 * head_dim)
    parts = partial_products(rows_here, tokens_here)
    parts = lax.all_to_all(parts, ring, split_axis=0, concat_axis=0, tiled=True)
    key_value = summed(parts, cosine, sine)
    row_kv = lax.all_gather(key_value, X_HI, axis=0)
    one_back = shifted(row_kv, CHIPS, 2)
    two_back = shifted(row_kv, CHIPS, 4)
    row_both = lax.all_gather(row_kv, CORE, axis=1)
    back_both = lax.all_gather(jnp.concatenate([two_back, one_back], axis=0), CORE, axis=1)
    offset = lax.axis_index(("x_hi", "core")) * local_count
    attention = attend(
        offset.astype(jnp.int32)[None],
        back_both.reshape(-1, 2 * head_dim),
        row_both.reshape(-1, 2 * head_dim),
        queries,
        first,
        cosine,
        sine,
    )
    return (attention, new_master, new_first, new_second)


def solution(mesh):
    finer = Mesh(mesh.devices.reshape(2, 16, 8, 2, 2), EVERY)
    rows = P(EVERY, None)
    placed = (rows, rows, P(EVERY), rows, rows, rows, rows, P())
    return jax.shard_map(
        compute,
        mesh=finer,
        in_specs=placed,
        out_specs=(rows, rows, rows, rows),
        check_vma=False,
    )
```

```python
import math

import jax
import jax.numpy as jnp
from jax import lax
from jax.experimental import pallas as pl
from jax.experimental.pallas import tpu as pltpu
from jax.sharding import Mesh
from jax.sharding import PartitionSpec as P


CORE = "core"
ALONG_X = ("x_lo", "x_hi")
ALONG_Y = "y"
ALONG_Z = "z"
X_HI = "x_hi"
EVERY = ("x_lo", "z", "y", "x_hi", "core")
CHIPS = ("x_lo", "z", "y", "x_hi")


beta_one = 0.9
beta_two = 0.95
learn_rate = 0.02
adam_eps = 1e-08
rope_base = 500000.0
masked_score = -1e30


def from_everyone(x, axis):
    copies = jnp.broadcast_to(x, (lax.axis_size(axis), *x.shape))
    return lax.all_to_all(copies, axis, split_axis=0, concat_axis=0, tiled=True)


def adam_update(grad, master, moment1, moment2, step):
    counter = step[0].astype(jnp.float32)
    new_first = beta_one * moment1 + (1.0 - beta_one) * grad
    new_second = beta_two * moment2 + (1.0 - beta_two) * grad * grad
    fixed_first = new_first / (1.0 - jnp.power(jnp.float32(beta_one), counter))
    fixed_second = new_second / (1.0 - jnp.power(jnp.float32(beta_two), counter))
    new_master = master - learn_rate * fixed_first / (jnp.sqrt(fixed_second) + adam_eps)
    return (new_master, new_first, new_second)


def on_chip(count):
    return [pl.BlockSpec(memory_space=pltpu.VMEM)] * count


def room(mib):
    return pltpu.CompilerParams(vmem_limit_bytes=mib * 2**20)


def split_kernel(tokens_ref, out_ref):
    span = 256
    source = lax.broadcasted_iota(jnp.int32, (span, span), 0)
    target = lax.broadcasted_iota(jnp.int32, (span, span), 1)
    goal = (((source >> 4) & 1) << 7) | ((source >> 5) << 4) | (source & 15)
    chosen = (goal == target).astype(jnp.float32).astype(jnp.bfloat16)
    count = tokens_ref.shape[0]
    for x_lo in range(2):
        for eight in range(2):
            first = (2 * x_lo + eight) * 8
            stacked = jnp.concatenate(
                [tokens_ref[:, part * span : (part + 1) * span] for part in range(first, first + 8)],
                axis=0,
            )
            moved = jnp.dot(stacked, chosen, preferred_element_type=jnp.float32)
            moved = moved.astype(jnp.bfloat16)
            for part in range(8):
                place = slice((8 * eight + part) * 128, (8 * eight + part + 1) * 128)
                for x_hi in range(2):
                    out_ref[x_lo + 2 * x_hi, :, place] = moved[
                        part * count : (part + 1) * count, x_hi * 128 : (x_hi + 1) * 128
                    ]


def split_columns(tokens):
    count, width = tokens.shape
    return pl.pallas_call(
        split_kernel,
        out_shape=jax.ShapeDtypeStruct((4, count, width // 4), tokens.dtype),
        in_specs=on_chip(1),
        out_specs=on_chip(1)[0],
        compiler_params=room(20),
        cost_estimate=pl.CostEstimate(
            flops=2 * count * width * 256, bytes_accessed=4 * count * width, transcendentals=0
        ),
    )(tokens)


def plane_product(mine_ref, theirs_ref, plane, halves, columns):
    depth = 16
    for half, half_ref in enumerate(halves):
        for y in range(4):
            for z in range(16):
                place = (z * 8 + 4 * half + y) * depth
                columns[place : place + depth] = half_ref[
                    (y * 16 + z) * depth : (y * 16 + z + 1) * depth
                ]
    rows = jnp.concatenate([mine_ref[plane], theirs_ref[plane]], axis=0)
    return jnp.dot(rows, columns[...], preferred_element_type=jnp.float32)


def own_kernel(place_ref, mine_ref, theirs_ref, low_ref, high_ref, out_ref, columns):
    out_ref[...] = plane_product(
        mine_ref, theirs_ref, place_ref[1], (low_ref, high_ref), columns
    )


def beside_kernel(
    place_ref, so_far_ref, mine_ref, theirs_ref, *pieces_and_out
):
    left_low, left_high, right_low, right_high, out_ref, columns, more = pieces_and_out
    left = (place_ref[1] + 3) & 3
    right = (place_ref[1] + 1) & 3
    out_ref[...] = (
        so_far_ref[...]
        + plane_product(mine_ref, theirs_ref, left, (left_low, left_high), columns)
        + plane_product(mine_ref, theirs_ref, right, (right_low, right_high), more)
    )


def across_kernel(
    place_ref, so_far_ref, mine_ref, theirs_ref, low_ref, high_ref, cosine_ref, sine_ref,
    out_ref, columns,
):
    across = (place_ref[1] + 2) & 3
    core = place_ref[0]
    total = so_far_ref[...] + plane_product(
        mine_ref, theirs_ref, across, (low_ref, high_ref), columns
    )
    count = mine_ref.shape[1]
    done = turned(total, cosine_ref[...], sine_ref[...]).astype(jnp.bfloat16)
    out_ref[pl.ds(pl.multiple_of(core * count, count), count)] = done[:count]
    out_ref[pl.ds(pl.multiple_of((1 - core) * count, count), count)] = done[count:]


def product(kernel, place, tiles, dtype, scratches, *operands):
    rows, width = tiles
    return pl.pallas_call(
        kernel,
        out_shape=jax.ShapeDtypeStruct(tiles, dtype),
        in_specs=[pl.BlockSpec(memory_space=pltpu.SMEM), *on_chip(len(operands))],
        out_specs=on_chip(1)[0],
        scratch_shapes=[pltpu.VMEM((2048, width), jnp.bfloat16)] * scratches,
        compiler_params=room(8),
        cost_estimate=pl.CostEstimate(
            flops=2 * rows * width * 2048 * scratches,
            bytes_accessed=2 * 2048 * (rows + width) * scratches,
            transcendentals=0,
        ),
    )(place, *operands)


def turned(values, cosine, sine):
    return values * cosine + pltpu.roll(values, values.shape[1] // 2, 1) * sine


def attend_kernel(
    offset_ref, back_ref, row_ref, queries_ref, first_ref, cosine_ref, sine_ref, out_ref, *windows
):
    count, width = queries_ref.shape
    head_dim = cosine_ref.shape[1]
    reach = back_ref.shape[1]
    seen = reach + count
    near = pl.ds(pl.multiple_of(offset_ref[0], 128), seen)
    for kind, window in enumerate(windows):
        window[:reach] = back_ref[kind]
        window[reach:] = row_ref[kind]
    keys, values = (window[near] for window in windows)
    row = lax.broadcasted_iota(jnp.int32, (count, head_dim), 0)
    column = lax.broadcasted_iota(jnp.int32, (count, head_dim), 1)
    first = first_ref[...]
    bias = jnp.concatenate(
        [
            jnp.where(
                (column + (start - reach) <= row) & (column + (start - reach) >= first),
                0.0,
                masked_score,
            )
            for start in range(0, seen, head_dim)
        ],
        axis=1,
    )
    cosine, sine = cosine_ref[...], sine_ref[...]
    scale = head_dim**-0.5 * math.log2(math.e)
    for head in range(width // head_dim):
        lanes = slice(head * head_dim, (head + 1) * head_dim)
        rows = turned(queries_ref[:, lanes].astype(jnp.float32), cosine, sine)
        scores = lax.dot_general(
            rows.astype(jnp.bfloat16),
            keys,
            (((1,), (1,)), ((), ())),
            preferred_element_type=jnp.float32,
        )
        scores = scores + bias
        top_score = jnp.max(scores, axis=1, keepdims=True)
        weights = jnp.exp2((scores - top_score) * scale)
        share = 1.0 / jnp.sum(weights, axis=1, keepdims=True)
        probs = (weights * share).astype(jnp.bfloat16)
        out_ref[:, lanes] = jnp.dot(
            probs, values, preferred_element_type=jnp.float32
        ).astype(jnp.bfloat16)


def attend(offset, back, row, queries, first, cosine, sine):
    count, width = queries.shape
    return pl.pallas_call(
        attend_kernel,
        out_shape=jax.ShapeDtypeStruct((count, width), jnp.bfloat16),
        in_specs=[pl.BlockSpec(memory_space=pltpu.SMEM), *on_chip(6)],
        out_specs=on_chip(1)[0],
        scratch_shapes=[pltpu.VMEM((back.shape[1] + row.shape[1], row.shape[2]), jnp.bfloat16)] * 2,
        compiler_params=room(20),
        cost_estimate=pl.CostEstimate(
            flops=4 * count * width * 1152,
            bytes_accessed=4 * count * width + 2 * back.size + 2 * row.size,
            transcendentals=count * width * 9,
        ),
    )(offset, back, row, queries, first, cosine, sine)


def rotation_tables(places, head_dim):
    half_width = head_dim // 2
    freqs = jnp.exp(
        jnp.arange(half_width, dtype=jnp.float32) * (-2.0 * math.log(rope_base) / head_dim)
    )
    angles = places.astype(jnp.float32)[:, None] * freqs
    cosine = jnp.cos(angles)
    sine = jnp.sin(angles)
    return (
        jnp.concatenate([cosine, cosine], axis=1),
        jnp.concatenate([-sine, sine], axis=1),
    )


def shifted(value, axis, steps):
    count = lax.axis_size(axis)
    return lax.ppermute(value, axis, [(source, source + steps) for source in range(count - steps)])


def along_x(value, steps):
    pairs = []
    for x_lo in range(2):
        for x_hi in range(2):
            goal = (2 * x_hi + x_lo + steps) % 4
            pairs.append((2 * x_lo + x_hi, 2 * (goal % 2) + goal // 2))
    return lax.ppermute(value, ALONG_X, pairs)


def column_halves(rows, axes):
    half = rows.shape[1] // 2
    for_core = jnp.stack([rows[:, :half], rows[:, half:]])
    reach = lax.axis_size(axes[0])
    copies = jnp.broadcast_to(for_core, (reach, *for_core.shape)).reshape(-1, *for_core.shape[1:])
    return lax.all_to_all(copies, axes, split_axis=0, concat_axis=0, tiled=True)


def compute(tokens, queries, positions, grad, master, moment1, moment2, step):
    head_dim = master.shape[1] // 2
    local_count = tokens.shape[0]
    core = lax.axis_index(CORE)
    place = jnp.stack([core, 2 * lax.axis_index(X_HI) + lax.axis_index("x_lo")]).astype(jnp.int32)
    new_master, new_first, new_second = adam_update(grad, master, moment1, moment2, step)
    weight = new_master.astype(jnp.bfloat16)
    over_z = column_halves(weight, (ALONG_Z, CORE)).reshape(-1, head_dim)
    mine = split_columns(tokens)
    theirs = lax.ppermute(mine, CORE, [(0, 1), (1, 0)])
    places_both = lax.all_gather(positions, CORE, axis=0, tiled=True)
    places_other = jnp.where(core == 0, places_both[local_count:], places_both[:local_count])
    cosine, sine = rotation_tables(positions, head_dim)
    cosine_other, sine_other = rotation_tables(places_other, head_dim)
    is_keys = core == 0
    key_cosine = jnp.where(is_keys, jnp.concatenate([cosine, cosine_other]), 1.0)
    key_sine = jnp.where(is_keys, jnp.concatenate([sine, sine_other]), 0.0)
    first = jnp.broadcast_to(
        (jnp.arange(local_count, dtype=jnp.int32) - positions)[:, None],
        (local_count, head_dim),
    )
    over_y = from_everyone(over_z, ALONG_Y).reshape(-1, head_dim)
    half = over_y.shape[0] // 2
    low, high = over_y[:half], over_y[half:]
    tiles = (2 * local_count, head_dim)
    left_low = along_x(low, 1)
    right_high = along_x(high, 3)
    left_high = along_x(high, 1)
    right_low = along_x(low, 3)
    so_far = product(own_kernel, place, tiles, jnp.float32, 1, mine, theirs, low, high)
    across_low = along_x(left_low, 1)
    across_high = along_x(right_high, 3)
    so_far = product(
        beside_kernel, place, tiles, jnp.float32, 2,
        so_far, mine, theirs, left_low, left_high, right_low, right_high,
    )
    half_kv = product(
        across_kernel, place, tiles, jnp.bfloat16, 1,
        so_far, mine, theirs, across_low, across_high, key_cosine, key_sine,
    )
    row_kv = lax.all_gather(half_kv, X_HI, axis=0, tiled=True)
    one_back = shifted(row_kv, CHIPS, 2)
    two_back = shifted(row_kv, CHIPS, 4)
    row_both = lax.all_gather(row_kv, CORE, axis=0)
    back_both = lax.all_gather(jnp.concatenate([two_back, one_back], axis=0), CORE, axis=0)
    offset = lax.axis_index(("x_hi", "core")) * local_count
    attention = attend(
        offset.astype(jnp.int32)[None], back_both, row_both, queries, first, cosine, sine
    )
    return (attention, new_master, new_first, new_second)


def solution(mesh):
    finer = Mesh(mesh.devices.reshape(2, 16, 8, 2, 2), EVERY)
    rows = P(EVERY, None)
    placed = (rows, rows, P(EVERY), rows, rows, rows, rows, P())
    return jax.shard_map(
        compute,
        mesh=finer,
        in_specs=placed,
        out_specs=(rows, rows, rows, rows),
        check_vma=False,
    )
```

```python
import math

import jax
import jax.numpy as jnp
from jax import lax
from jax.experimental import pallas as pl
from jax.experimental.pallas import tpu as pltpu
from jax.sharding import Mesh
from jax.sharding import PartitionSpec as P


CORE = "core"
ALONG_X = ("x_lo", "x_hi")
ALONG_Y = "y"
ALONG_Z = "z"
X_HI = "x_hi"
EVERY = ("x_lo", "z", "y", "x_hi", "core")
CHIPS = ("x_lo", "z", "y", "x_hi")


beta_one = 0.9
beta_two = 0.95
learn_rate = 0.02
adam_eps = 1e-08
rope_base = 500000.0
masked_score = -1e30


def from_everyone(x, axis):
    copies = jnp.broadcast_to(x, (lax.axis_size(axis), *x.shape))
    return lax.all_to_all(copies, axis, split_axis=0, concat_axis=0, tiled=True)


def adam_update(grad, master, moment1, moment2, step):
    counter = step[0].astype(jnp.float32)
    new_first = beta_one * moment1 + (1.0 - beta_one) * grad
    new_second = beta_two * moment2 + (1.0 - beta_two) * grad * grad
    fixed_first = new_first / (1.0 - jnp.power(jnp.float32(beta_one), counter))
    fixed_second = new_second / (1.0 - jnp.power(jnp.float32(beta_two), counter))
    new_master = master - learn_rate * fixed_first / (jnp.sqrt(fixed_second) + adam_eps)
    return (new_master, new_first, new_second)


def on_chip(count):
    return [pl.BlockSpec(memory_space=pltpu.VMEM)] * count


def room(mib):
    return pltpu.CompilerParams(vmem_limit_bytes=mib * 2**20)


def split_kernel(tokens_ref, out_ref):
    span = 256
    source = lax.broadcasted_iota(jnp.int32, (span, span), 0)
    target = lax.broadcasted_iota(jnp.int32, (span, span), 1)
    goal = (((source >> 4) & 1) << 7) | ((source >> 5) << 4) | (source & 15)
    chosen = (goal == target).astype(jnp.float32).astype(jnp.bfloat16)
    count = tokens_ref.shape[0]
    for x_lo in range(2):
        for eight in range(2):
            first = (2 * x_lo + eight) * 8
            stacked = jnp.concatenate(
                [tokens_ref[:, part * span : (part + 1) * span] for part in range(first, first + 8)],
                axis=0,
            )
            moved = jnp.dot(stacked, chosen, preferred_element_type=jnp.float32)
            moved = moved.astype(jnp.bfloat16)
            for part in range(8):
                place = slice((8 * eight + part) * 128, (8 * eight + part + 1) * 128)
                for x_hi in range(2):
                    out_ref[x_lo + 2 * x_hi, :, place] = moved[
                        part * count : (part + 1) * count, x_hi * 128 : (x_hi + 1) * 128
                    ]


def split_columns(tokens):
    count, width = tokens.shape
    return pl.pallas_call(
        split_kernel,
        out_shape=jax.ShapeDtypeStruct((4, count, width // 4), tokens.dtype),
        in_specs=on_chip(1),
        out_specs=on_chip(1)[0],
        compiler_params=room(20),
        cost_estimate=pl.CostEstimate(
            flops=2 * count * width * 256, bytes_accessed=4 * count * width, transcendentals=0
        ),
    )(tokens)


def plane_product(mine_ref, theirs_ref, plane, pieces, columns, held, arrival):
    fetch = pltpu.make_async_copy(theirs_ref.at[plane], held, arrival)
    fetch.start()
    depth, along_y = 16, 8 // len(pieces)
    for order, piece_ref in enumerate(pieces):
        for y in range(along_y):
            for z in range(16):
                place = (z * 8 + along_y * order + y) * depth
                columns[place : place + depth] = piece_ref[
                    (y * 16 + z) * depth : (y * 16 + z + 1) * depth
                ]
    own = jnp.dot(mine_ref[plane], columns[...], preferred_element_type=jnp.float32)
    fetch.wait()
    other = jnp.dot(held[...], columns[...], preferred_element_type=jnp.float32)
    return jnp.concatenate([own, other], axis=0)


def own_kernel(place_ref, theirs_ref, mine_ref, piece_ref, out_ref, columns, held, arrival):
    out_ref[...] = plane_product(
        mine_ref, theirs_ref, place_ref[1], (piece_ref,), columns, held, arrival
    )


def beside_kernel(
    place_ref, theirs_ref, mine_ref, so_far_ref, left_ref, right_ref, out_ref, *scratches
):
    left = (place_ref[1] + 3) & 3
    right = (place_ref[1] + 1) & 3
    from_left = plane_product(mine_ref, theirs_ref, left, (left_ref,), *scratches[0::2])
    from_right = plane_product(mine_ref, theirs_ref, right, (right_ref,), *scratches[1::2])
    out_ref[...] = so_far_ref[...] + from_left + from_right


def across_kernel(
    place_ref, theirs_ref, mine_ref, so_far_ref, low_ref, high_ref, cosine_ref, sine_ref,
    out_ref, columns, held, arrival,
):
    across = (place_ref[1] + 2) & 3
    core = place_ref[0]
    total = so_far_ref[...] + plane_product(
        mine_ref, theirs_ref, across, (low_ref, high_ref), columns, held, arrival
    )
    count = mine_ref.shape[1]
    done = turned(total, cosine_ref[...], sine_ref[...]).astype(jnp.bfloat16)
    out_ref[pl.ds(pl.multiple_of(core * count, count), count)] = done[:count]
    out_ref[pl.ds(pl.multiple_of((1 - core) * count, count), count)] = done[count:]


def product(kernel, place, theirs, mine, tiles, dtype, planes, *operands):
    rows, width = tiles
    depth = mine.shape[2]
    return pl.pallas_call(
        kernel,
        out_shape=jax.ShapeDtypeStruct(tiles, dtype),
        in_specs=[
            pl.BlockSpec(memory_space=pltpu.SMEM),
            pl.BlockSpec(memory_space=pl.ANY),
            *on_chip(len(operands) + 1),
        ],
        out_specs=on_chip(1)[0],
        scratch_shapes=[
            *[pltpu.VMEM((depth, width), jnp.bfloat16)] * planes,
            *[pltpu.VMEM(mine.shape[1:], jnp.bfloat16)] * planes,
            *[pltpu.SemaphoreType.DMA] * planes,
        ],
        compiler_params=room(8),
        cost_estimate=pl.CostEstimate(
            flops=2 * rows * width * depth * planes,
            bytes_accessed=2 * depth * (rows + width) * planes,
            transcendentals=0,
        ),
    )(place, theirs, mine, *operands)


def turned(values, cosine, sine):
    return values * cosine + pltpu.roll(values, values.shape[1] // 2, 1) * sine


def attend_kernel(
    offset_ref, far_ref, near_ref, queries_ref, first_ref, cosine_ref, sine_ref, out_ref, *windows
):
    count, width = queries_ref.shape
    head_dim = cosine_ref.shape[1]
    held = far_ref.shape[1]
    seen = windows[0].shape[0] - count
    reach = seen - count
    near = pl.ds(pl.multiple_of(offset_ref[0], 128), seen)
    for kind, window in enumerate(windows):
        window[:held] = far_ref[kind]
        window[held:] = near_ref[kind]
    keys, values = (window[near] for window in windows)
    row = lax.broadcasted_iota(jnp.int32, (count, head_dim), 0)
    column = lax.broadcasted_iota(jnp.int32, (count, head_dim), 1)
    first = first_ref[...]
    bias = jnp.concatenate(
        [
            jnp.where(
                (column + (start - reach) <= row) & (column + (start - reach) >= first),
                0.0,
                masked_score,
            )
            for start in range(0, seen, head_dim)
        ],
        axis=1,
    )
    cosine, sine = cosine_ref[...], sine_ref[...]
    scale = head_dim**-0.5 * math.log2(math.e)
    for head in range(width // head_dim):
        lanes = slice(head * head_dim, (head + 1) * head_dim)
        rows = turned(queries_ref[:, lanes].astype(jnp.float32), cosine, sine)
        scores = lax.dot_general(
            rows.astype(jnp.bfloat16),
            keys,
            (((1,), (1,)), ((), ())),
            preferred_element_type=jnp.float32,
        )
        scores = scores + bias
        top_score = jnp.max(scores, axis=1, keepdims=True)
        weights = jnp.exp2((scores - top_score) * scale)
        share = 1.0 / jnp.sum(weights, axis=1, keepdims=True)
        probs = (weights * share).astype(jnp.bfloat16)
        out_ref[:, lanes] = jnp.dot(
            probs, values, preferred_element_type=jnp.float32
        ).astype(jnp.bfloat16)


def attend(offset, far, close, queries, first, cosine, sine):
    count, width = queries.shape
    return pl.pallas_call(
        attend_kernel,
        out_shape=jax.ShapeDtypeStruct((count, width), jnp.bfloat16),
        in_specs=[pl.BlockSpec(memory_space=pltpu.SMEM), *on_chip(6)],
        out_specs=on_chip(1)[0],
        scratch_shapes=[pltpu.VMEM((far.shape[1] + close.shape[1], close.shape[2]), jnp.bfloat16)] * 2,
        compiler_params=room(20),
        cost_estimate=pl.CostEstimate(
            flops=4 * count * width * 1152,
            bytes_accessed=4 * count * width + 2 * far.size + 2 * close.size,
            transcendentals=count * width * 9,
        ),
    )(offset, far, close, queries, first, cosine, sine)


def rotation_tables(places, head_dim):
    half_width = head_dim // 2
    freqs = jnp.exp(
        jnp.arange(half_width, dtype=jnp.float32) * (-2.0 * math.log(rope_base) / head_dim)
    )
    angles = places.astype(jnp.float32)[:, None] * freqs
    cosine = jnp.cos(angles)
    sine = jnp.sin(angles)
    return (
        jnp.concatenate([cosine, cosine], axis=1),
        jnp.concatenate([-sine, sine], axis=1),
    )


def shifted(value, axis, steps):
    count = lax.axis_size(axis)
    return lax.ppermute(value, axis, [(source, source + steps) for source in range(count - steps)])


def along_x(value, steps):
    pairs = []
    for x_lo in range(2):
        for x_hi in range(2):
            goal = (2 * x_hi + x_lo + steps) % 4
            pairs.append((2 * x_lo + x_hi, 2 * (goal % 2) + goal // 2))
    return lax.ppermute(value, ALONG_X, pairs)


def column_halves(rows, axes):
    half = rows.shape[1] // 2
    for_core = jnp.stack([rows[:, :half], rows[:, half:]])
    reach = lax.axis_size(axes[0])
    copies = jnp.broadcast_to(for_core, (reach, *for_core.shape)).reshape(-1, *for_core.shape[1:])
    return lax.all_to_all(copies, axes, split_axis=0, concat_axis=0, tiled=True)


def compute(tokens, queries, positions, grad, master, moment1, moment2, step):
    head_dim = master.shape[1] // 2
    local_count = tokens.shape[0]
    core = lax.axis_index(CORE)
    place = jnp.stack([core, 2 * lax.axis_index(X_HI) + lax.axis_index("x_lo")]).astype(jnp.int32)
    new_master, new_first, new_second = adam_update(grad, master, moment1, moment2, step)
    weight = new_master.astype(jnp.bfloat16)
    over_z = column_halves(weight, (ALONG_Z, CORE)).reshape(-1, head_dim)
    mine = split_columns(tokens)
    theirs = lax.ppermute(mine, CORE, [(0, 1), (1, 0)])
    places_both = lax.all_gather(positions, CORE, axis=0, tiled=True)
    places_other = jnp.where(core == 0, places_both[local_count:], places_both[:local_count])
    cosine, sine = rotation_tables(positions, head_dim)
    cosine_other, sine_other = rotation_tables(places_other, head_dim)
    is_keys = core == 0
    key_cosine = jnp.where(is_keys, jnp.concatenate([cosine, cosine_other]), 1.0)
    key_sine = jnp.where(is_keys, jnp.concatenate([sine, sine_other]), 0.0)
    first = jnp.broadcast_to(
        (jnp.arange(local_count, dtype=jnp.int32) - positions)[:, None],
        (local_count, head_dim),
    )
    over_y = from_everyone(over_z, ALONG_Y).reshape(-1, head_dim)
    half = over_y.shape[0] // 2
    tiles = (2 * local_count, head_dim)
    left = along_x(over_y, 1)
    right = along_x(over_y, 3)
    so_far = product(own_kernel, place, theirs, mine, tiles, jnp.float32, 1, over_y)
    across_low = along_x(left[:half], 1)
    across_high = along_x(right[half:], 3)
    so_far = product(beside_kernel, place, theirs, mine, tiles, jnp.float32, 2, so_far, left, right)
    half_kv = product(
        across_kernel, place, theirs, mine, tiles, jnp.bfloat16, 1,
        so_far, across_low, across_high, key_cosine, key_sine,
    )
    one_back = shifted(half_kv, CHIPS, 1)
    two_back = shifted(half_kv, CHIPS, 2)
    near_half = jnp.concatenate([two_back, one_back], axis=0)
    far_half = shifted(near_half, CHIPS, 2)
    near_both = lax.all_gather(
        jnp.concatenate([near_half, half_kv], axis=0), CORE, axis=0
    )
    far_both = lax.all_gather(far_half, CORE, axis=0)
    offset = core * local_count
    attention = attend(
        offset.astype(jnp.int32)[None], far_both, near_both, queries, first, cosine, sine
    )
    return (attention, new_master, new_first, new_second)


def solution(mesh):
    finer = Mesh(mesh.devices.reshape(2, 16, 8, 2, 2), EVERY)
    rows = P(EVERY, None)
    placed = (rows, rows, P(EVERY), rows, rows, rows, rows, P())
    return jax.shard_map(
        compute,
        mesh=finer,
        in_specs=placed,
        out_specs=(rows, rows, rows, rows),
        check_vma=False,
    )
```

```python
import math

import jax
import jax.numpy as jnp
from jax import lax
from jax.experimental import pallas as pl
from jax.experimental.pallas import tpu as pltpu
from jax.sharding import Mesh
from jax.sharding import PartitionSpec as P


CORE = "core"
ALONG_X = ("x_lo", "x_hi")
ALONG_Y = "y"
ALONG_Z = "z"
X_HI = "x_hi"
EVERY = ("x_lo", "z", "y", "x_hi", "core")
CHIPS = ("x_lo", "z", "y", "x_hi")


beta_one = 0.9
beta_two = 0.95
learn_rate = 0.02
adam_eps = 1e-08
rope_base = 500000.0
masked_score = -1e30


def from_everyone(x, axis):
    copies = jnp.broadcast_to(x, (lax.axis_size(axis), *x.shape))
    return lax.all_to_all(copies, axis, split_axis=0, concat_axis=0, tiled=True)


def adam_update(grad, master, moment1, moment2, step):
    counter = step[0].astype(jnp.float32)
    new_first = beta_one * moment1 + (1.0 - beta_one) * grad
    new_second = beta_two * moment2 + (1.0 - beta_two) * grad * grad
    fixed_first = new_first / (1.0 - jnp.power(jnp.float32(beta_one), counter))
    fixed_second = new_second / (1.0 - jnp.power(jnp.float32(beta_two), counter))
    new_master = master - learn_rate * fixed_first / (jnp.sqrt(fixed_second) + adam_eps)
    return (new_master, new_first, new_second)


def on_chip(count):
    return [pl.BlockSpec(memory_space=pltpu.VMEM)] * count


def room(mib):
    return pltpu.CompilerParams(vmem_limit_bytes=mib * 2**20)


def split_kernel(tokens_ref, out_ref):
    span = 256
    source = lax.broadcasted_iota(jnp.int32, (span, span), 0)
    target = lax.broadcasted_iota(jnp.int32, (span, span), 1)
    goal = (((source >> 4) & 1) << 7) | ((source >> 5) << 4) | (source & 15)
    chosen = (goal == target).astype(jnp.float32).astype(jnp.bfloat16)
    count = tokens_ref.shape[0]
    for x_lo in range(2):
        for eight in range(2):
            first = (2 * x_lo + eight) * 8
            stacked = jnp.concatenate(
                [tokens_ref[:, part * span : (part + 1) * span] for part in range(first, first + 8)],
                axis=0,
            )
            moved = jnp.dot(stacked, chosen, preferred_element_type=jnp.float32)
            moved = moved.astype(jnp.bfloat16)
            for part in range(8):
                place = slice((8 * eight + part) * 128, (8 * eight + part + 1) * 128)
                for x_hi in range(2):
                    out_ref[x_lo + 2 * x_hi, :, place] = moved[
                        part * count : (part + 1) * count, x_hi * 128 : (x_hi + 1) * 128
                    ]


def split_columns(tokens):
    count, width = tokens.shape
    return pl.pallas_call(
        split_kernel,
        out_shape=jax.ShapeDtypeStruct((4, count, width // 4), tokens.dtype),
        in_specs=on_chip(1),
        out_specs=on_chip(1)[0],
        compiler_params=room(20),
        cost_estimate=pl.CostEstimate(
            flops=2 * count * width * 256, bytes_accessed=4 * count * width, transcendentals=0
        ),
    )(tokens)


def plane_fetch(theirs_ref, plane, held, arrival):
    fetch = pltpu.make_async_copy(theirs_ref.at[plane], held, arrival)
    fetch.start()
    return fetch


def plane_product(mine_ref, plane, pieces, columns, held, fetch):
    depth, along_y = 16, 8 // len(pieces)
    for order, piece_ref in enumerate(pieces):
        for y in range(along_y):
            for z in range(16):
                place = (z * 8 + along_y * order + y) * depth
                columns[place : place + depth] = piece_ref[
                    (y * 16 + z) * depth : (y * 16 + z + 1) * depth
                ]
    own = jnp.dot(mine_ref[plane], columns[...], preferred_element_type=jnp.float32)
    fetch.wait()
    other = jnp.dot(held[...], columns[...], preferred_element_type=jnp.float32)
    return jnp.concatenate([own, other], axis=0)


def own_kernel(place_ref, theirs_ref, mine_ref, piece_ref, out_ref, columns, held, arrival):
    plane = place_ref[1]
    fetch = plane_fetch(theirs_ref, plane, held, arrival)
    out_ref[...] = plane_product(mine_ref, plane, (piece_ref,), columns, held, fetch)


def beside_kernel(
    place_ref, theirs_ref, mine_ref, so_far_ref, left_ref, right_ref, out_ref,
    columns, more, held, also, arrival, later,
):
    left = (place_ref[1] + 3) & 3
    right = (place_ref[1] + 1) & 3
    fetch = plane_fetch(theirs_ref, left, held, arrival)
    other_fetch = plane_fetch(theirs_ref, right, also, later)
    from_left = plane_product(mine_ref, left, (left_ref,), columns, held, fetch)
    from_right = plane_product(mine_ref, right, (right_ref,), more, also, other_fetch)
    out_ref[...] = so_far_ref[...] + from_left + from_right


def across_kernel(
    place_ref, theirs_ref, mine_ref, so_far_ref, low_ref, high_ref, cosine_ref, sine_ref,
    out_ref, columns, held, arrival,
):
    across = (place_ref[1] + 2) & 3
    core = place_ref[0]
    fetch = plane_fetch(theirs_ref, across, held, arrival)
    total = so_far_ref[...] + plane_product(
        mine_ref, across, (low_ref, high_ref), columns, held, fetch
    )
    count = mine_ref.shape[1]
    done = turned(total, cosine_ref[...], sine_ref[...]).astype(jnp.bfloat16)
    out_ref[pl.ds(pl.multiple_of(core * count, count), count)] = done[:count]
    out_ref[pl.ds(pl.multiple_of((1 - core) * count, count), count)] = done[count:]


def product(kernel, place, theirs, mine, tiles, dtype, planes, *operands):
    rows, width = tiles
    depth = mine.shape[2]
    return pl.pallas_call(
        kernel,
        out_shape=jax.ShapeDtypeStruct(tiles, dtype),
        in_specs=[
            pl.BlockSpec(memory_space=pltpu.SMEM),
            pl.BlockSpec(memory_space=pl.ANY),
            *on_chip(len(operands) + 1),
        ],
        out_specs=on_chip(1)[0],
        scratch_shapes=[
            *[pltpu.VMEM((depth, width), jnp.bfloat16)] * planes,
            *[pltpu.VMEM(mine.shape[1:], jnp.bfloat16)] * planes,
            *[pltpu.SemaphoreType.DMA] * planes,
        ],
        compiler_params=room(8),
        cost_estimate=pl.CostEstimate(
            flops=2 * rows * width * depth * planes,
            bytes_accessed=2 * depth * (rows + width) * planes,
            transcendentals=0,
        ),
    )(place, theirs, mine, *operands)


def turned(values, cosine, sine):
    return values * cosine + pltpu.roll(values, values.shape[1] // 2, 1) * sine


def attend_kernel(
    offset_ref, far_ref, near_ref, queries_ref, first_ref, cosine_ref, sine_ref, out_ref, *windows
):
    count, width = queries_ref.shape
    head_dim = cosine_ref.shape[1]
    held = far_ref.shape[1]
    reach = held
    seen = reach + count
    near = pl.ds(pl.multiple_of(offset_ref[0], 128), seen)
    for kind, window in enumerate(windows):
        window[:held] = far_ref[kind]
        window[held:] = near_ref[kind]
    keys, values = (window[near] for window in windows)
    token = lax.broadcasted_iota(jnp.int32, (seen, count), 0) - reach
    query = lax.broadcasted_iota(jnp.int32, (seen, count), 1)
    allowed = (token <= query) & (token >= first_ref[0:1, :])
    bias = jnp.where(allowed, 0.0, masked_score).astype(jnp.bfloat16)
    keys = jnp.concatenate([keys, bias], axis=1)
    row = lax.broadcasted_iota(jnp.int32, (count, count), 0)
    column = lax.broadcasted_iota(jnp.int32, (count, count), 1)
    unit = (row == column).astype(jnp.float32).astype(jnp.bfloat16)
    cosine, sine = cosine_ref[...], sine_ref[...]
    scale = head_dim**-0.5 * math.log2(math.e)
    heads = width // head_dim
    for start in range(0, heads, 4):
        rows = jnp.concatenate(
            [
                jnp.concatenate(
                    [
                        turned(
                            queries_ref[:, h * head_dim : (h + 1) * head_dim].astype(jnp.float32),
                            cosine,
                            sine,
                        ).astype(jnp.bfloat16),
                        unit,
                    ],
                    axis=1,
                )
                for h in range(start, start + 4)
            ],
            axis=0,
        )
        scores = lax.dot_general(
            rows, keys, (((1,), (1,)), ((), ())), preferred_element_type=jnp.float32
        )
        top_score = jnp.max(scores, axis=1, keepdims=True)
        weights = jnp.exp2((scores - top_score) * scale)
        share = 1.0 / jnp.sum(weights, axis=1, keepdims=True)
        probs = (weights * share).astype(jnp.bfloat16)
        result = jnp.dot(probs, values, preferred_element_type=jnp.float32).astype(jnp.bfloat16)
        for h in range(4):
            out_ref[:, (start + h) * head_dim : (start + h + 1) * head_dim] = result[
                h * count : (h + 1) * count
            ]


def attend(offset, far, close, queries, first, cosine, sine):
    count, width = queries.shape
    return pl.pallas_call(
        attend_kernel,
        out_shape=jax.ShapeDtypeStruct((count, width), jnp.bfloat16),
        in_specs=[pl.BlockSpec(memory_space=pltpu.SMEM), *on_chip(6)],
        out_specs=on_chip(1)[0],
        scratch_shapes=[pltpu.VMEM((far.shape[1] + close.shape[1], close.shape[2]), jnp.bfloat16)] * 2,
        compiler_params=room(20),
        cost_estimate=pl.CostEstimate(
            flops=6 * count * width * 1152,
            bytes_accessed=4 * count * width + 2 * far.size + 2 * close.size,
            transcendentals=count * width * 9,
        ),
    )(offset, far, close, queries, first, cosine, sine)


def rotation_tables(places, head_dim):
    half_width = head_dim // 2
    freqs = jnp.exp(
        jnp.arange(half_width, dtype=jnp.float32) * (-2.0 * math.log(rope_base) / head_dim)
    )
    angles = places.astype(jnp.float32)[:, None] * freqs
    cosine = jnp.cos(angles)
    sine = jnp.sin(angles)
    return (
        jnp.concatenate([cosine, cosine], axis=1),
        jnp.concatenate([-sine, sine], axis=1),
    )


def shifted(value, axis, steps):
    count = lax.axis_size(axis)
    return lax.ppermute(value, axis, [(source, source + steps) for source in range(count - steps)])


def along_x(value, steps):
    pairs = []
    for x_lo in range(2):
        for x_hi in range(2):
            goal = (2 * x_hi + x_lo + steps) % 4
            pairs.append((2 * x_lo + x_hi, 2 * (goal % 2) + goal // 2))
    return lax.ppermute(value, ALONG_X, pairs)


def column_halves(rows, axes):
    half = rows.shape[1] // 2
    for_core = jnp.stack([rows[:, :half], rows[:, half:]])
    reach = lax.axis_size(axes[0])
    copies = jnp.broadcast_to(for_core, (reach, *for_core.shape)).reshape(-1, *for_core.shape[1:])
    return lax.all_to_all(copies, axes, split_axis=0, concat_axis=0, tiled=True)


def compute(tokens, queries, positions, grad, master, moment1, moment2, step):
    head_dim = master.shape[1] // 2
    local_count = tokens.shape[0]
    core = lax.axis_index(CORE)
    place = jnp.stack([core, 2 * lax.axis_index(X_HI) + lax.axis_index("x_lo")]).astype(jnp.int32)
    new_master, new_first, new_second = adam_update(grad, master, moment1, moment2, step)
    weight = new_master.astype(jnp.bfloat16)
    over_z = column_halves(weight, (ALONG_Z, CORE)).reshape(-1, head_dim)
    mine = split_columns(tokens)
    theirs = lax.ppermute(mine, CORE, [(0, 1), (1, 0)])
    places_both = lax.all_gather(positions, CORE, axis=0, tiled=True)
    places_other = jnp.where(core == 0, places_both[local_count:], places_both[:local_count])
    cosine, sine = rotation_tables(positions, head_dim)
    cosine_other, sine_other = rotation_tables(places_other, head_dim)
    is_keys = core == 0
    key_cosine = jnp.where(is_keys, jnp.concatenate([cosine, cosine_other]), 1.0)
    key_sine = jnp.where(is_keys, jnp.concatenate([sine, sine_other]), 0.0)
    first = jnp.broadcast_to(
        (jnp.arange(local_count, dtype=jnp.int32) - positions)[None, :], (8, local_count)
    )
    over_y = from_everyone(over_z, ALONG_Y).reshape(-1, head_dim)
    half = over_y.shape[0] // 2
    tiles = (2 * local_count, head_dim)
    left = along_x(over_y, 1)
    right = along_x(over_y, 3)
    so_far = product(own_kernel, place, theirs, mine, tiles, jnp.float32, 1, over_y)
    across_low = along_x(left[:half], 1)
    across_high = along_x(right[half:], 3)
    so_far = product(beside_kernel, place, theirs, mine, tiles, jnp.float32, 2, so_far, left, right)
    half_kv = product(
        across_kernel, place, theirs, mine, tiles, jnp.bfloat16, 1,
        so_far, across_low, across_high, key_cosine, key_sine,
    )
    row_kv = lax.all_gather(half_kv, X_HI, axis=0, tiled=True)
    one_back = shifted(row_kv, CHIPS, 2)
    two_back = shifted(row_kv, CHIPS, 4)
    near_both = lax.all_gather(row_kv, CORE, axis=0)
    far_both = lax.all_gather(jnp.concatenate([two_back, one_back], axis=0), CORE, axis=0)
    offset = lax.axis_index(("x_hi", "core")) * local_count
    attention = attend(
        offset.astype(jnp.int32)[None], far_both, near_both, queries, first, cosine, sine
    )
    return (attention, new_master, new_first, new_second)


def solution(mesh):
    finer = Mesh(mesh.devices.reshape(2, 16, 8, 2, 2), EVERY)
    rows = P(EVERY, None)
    placed = (rows, rows, P(EVERY), rows, rows, rows, rows, P())
    return jax.shard_map(
        compute,
        mesh=finer,
        in_specs=placed,
        out_specs=(rows, rows, rows, rows),
        check_vma=False,
    )
```

```python
import math

import jax
import jax.numpy as jnp
from jax import lax
from jax.experimental import pallas as pl
from jax.experimental.pallas import tpu as pltpu
from jax.sharding import Mesh
from jax.sharding import PartitionSpec as P


CORE = "core"
ALONG_X = ("x_lo", "x_hi")
ALONG_Y = "y"
ALONG_Z = "z"
X_HI = "x_hi"
EVERY = ("x_lo", "z", "y", "x_hi", "core")
CHIPS = ("x_lo", "z", "y", "x_hi")


beta_one = 0.9
beta_two = 0.95
learn_rate = 0.02
adam_eps = 1e-08
rope_base = 500000.0
masked_score = -1e30


def adam_update(grad, master, moment1, moment2, step):
    counter = step[0].astype(jnp.float32)
    new_first = beta_one * moment1 + (1.0 - beta_one) * grad
    new_second = beta_two * moment2 + (1.0 - beta_two) * grad * grad
    fixed_first = new_first / (1.0 - jnp.power(jnp.float32(beta_one), counter))
    fixed_second = new_second / (1.0 - jnp.power(jnp.float32(beta_two), counter))
    new_master = master - learn_rate * fixed_first / (jnp.sqrt(fixed_second) + adam_eps)
    return (new_master, new_first, new_second)


def on_chip(count):
    return [pl.BlockSpec(memory_space=pltpu.VMEM)] * count


def room(mib):
    return pltpu.CompilerParams(vmem_limit_bytes=mib * 2**20)


def split_kernel(tokens_ref, out_ref):
    span = 256
    source = lax.broadcasted_iota(jnp.int32, (span, span), 0)
    target = lax.broadcasted_iota(jnp.int32, (span, span), 1)
    goal = (((source >> 4) & 1) << 7) | ((source >> 5) << 4) | (source & 15)
    chosen = (goal == target).astype(jnp.float32).astype(jnp.bfloat16)
    count = tokens_ref.shape[0]
    for x_lo in range(2):
        for eight in range(2):
            first = (2 * x_lo + eight) * 8
            stacked = jnp.concatenate(
                [tokens_ref[:, part * span : (part + 1) * span] for part in range(first, first + 8)],
                axis=0,
            )
            moved = jnp.dot(stacked, chosen, preferred_element_type=jnp.float32)
            moved = moved.astype(jnp.bfloat16)
            for part in range(8):
                place = slice((8 * eight + part) * 128, (8 * eight + part + 1) * 128)
                for x_hi in range(2):
                    out_ref[x_lo + 2 * x_hi, :, place] = moved[
                        part * count : (part + 1) * count, x_hi * 128 : (x_hi + 1) * 128
                    ]


def split_columns(tokens):
    count, width = tokens.shape
    return pl.pallas_call(
        split_kernel,
        out_shape=jax.ShapeDtypeStruct((4, count, width // 4), tokens.dtype),
        in_specs=on_chip(1),
        out_specs=on_chip(1)[0],
        compiler_params=room(20),
        cost_estimate=pl.CostEstimate(
            flops=2 * count * width * 256, bytes_accessed=4 * count * width, transcendentals=0
        ),
    )(tokens)


def plane_fetch(theirs_ref, plane, held, arrival):
    fetch = pltpu.make_async_copy(theirs_ref.at[plane], held, arrival)
    fetch.start()
    return fetch


def plane_product(mine_ref, plane, pieces, columns, held, fetch):
    depth, along_y = 16, 8 // len(pieces)
    for order, piece_ref in enumerate(pieces):
        for y in range(along_y):
            for z in range(16):
                place = (z * 8 + along_y * order + y) * depth
                columns[place : place + depth] = piece_ref[
                    (y * 16 + z) * depth : (y * 16 + z + 1) * depth
                ]
    own = jnp.dot(mine_ref[plane], columns[...], preferred_element_type=jnp.float32)
    fetch.wait()
    other = jnp.dot(held[...], columns[...], preferred_element_type=jnp.float32)
    return jnp.concatenate([own, other], axis=0)


def own_kernel(place_ref, theirs_ref, mine_ref, piece_ref, out_ref, columns, held, arrival):
    plane = place_ref[1]
    fetch = plane_fetch(theirs_ref, plane, held, arrival)
    out_ref[...] = plane_product(mine_ref, plane, (piece_ref,), columns, held, fetch)


def beside_kernel(
    place_ref, theirs_ref, mine_ref, so_far_ref, left_ref, right_ref, out_ref,
    columns, more, held, also, arrival, later,
):
    left = (place_ref[1] + 3) & 3
    right = (place_ref[1] + 1) & 3
    fetch = plane_fetch(theirs_ref, left, held, arrival)
    other_fetch = plane_fetch(theirs_ref, right, also, later)
    from_left = plane_product(mine_ref, left, (left_ref,), columns, held, fetch)
    from_right = plane_product(mine_ref, right, (right_ref,), more, also, other_fetch)
    out_ref[...] = so_far_ref[...] + from_left + from_right


def across_kernel(
    place_ref, theirs_ref, mine_ref, so_far_ref, low_ref, high_ref, cosine_ref, sine_ref,
    out_ref, columns, held, arrival,
):
    across = (place_ref[1] + 2) & 3
    core = place_ref[0]
    fetch = plane_fetch(theirs_ref, across, held, arrival)
    total = so_far_ref[...] + plane_product(
        mine_ref, across, (low_ref, high_ref), columns, held, fetch
    )
    count = mine_ref.shape[1]
    done = turned(total, cosine_ref[...], sine_ref[...]).astype(jnp.bfloat16)
    out_ref[pl.ds(pl.multiple_of(core * count, count), count)] = done[:count]
    out_ref[pl.ds(pl.multiple_of((1 - core) * count, count), count)] = done[count:]


def product(kernel, place, theirs, mine, tiles, dtype, planes, *operands):
    rows, width = tiles
    depth = mine.shape[2]
    return pl.pallas_call(
        kernel,
        out_shape=jax.ShapeDtypeStruct(tiles, dtype),
        in_specs=[
            pl.BlockSpec(memory_space=pltpu.SMEM),
            pl.BlockSpec(memory_space=pl.ANY),
            *on_chip(len(operands) + 1),
        ],
        out_specs=on_chip(1)[0],
        scratch_shapes=[
            *[pltpu.VMEM((depth, width), jnp.bfloat16)] * planes,
            *[pltpu.VMEM(mine.shape[1:], jnp.bfloat16)] * planes,
            *[pltpu.SemaphoreType.DMA] * planes,
        ],
        compiler_params=room(8),
        cost_estimate=pl.CostEstimate(
            flops=2 * rows * width * depth * planes,
            bytes_accessed=2 * depth * (rows + width) * planes,
            transcendentals=0,
        ),
    )(place, theirs, mine, *operands)


def turned(values, cosine, sine):
    return values * cosine + pltpu.roll(values, values.shape[1] // 2, 1) * sine


def attend_kernel(
    offset_ref, far_ref, near_ref, queries_ref, first_ref, cosine_ref, sine_ref, out_ref, *windows
):
    count, width = queries_ref.shape
    head_dim = cosine_ref.shape[1]
    held = far_ref.shape[1]
    reach = held
    seen = reach + count
    near = pl.ds(pl.multiple_of(offset_ref[0], 128), seen)
    for kind, window in enumerate(windows):
        window[:held] = far_ref[kind]
        window[held:] = near_ref[kind]
    keys, values = (window[near] for window in windows)
    token = lax.broadcasted_iota(jnp.int32, (seen, count), 0) - reach
    query = lax.broadcasted_iota(jnp.int32, (seen, count), 1)
    allowed = (token <= query) & (token >= first_ref[0:1, :])
    bias = jnp.where(allowed, 0.0, masked_score).astype(jnp.bfloat16)
    keys = jnp.concatenate([keys, bias], axis=1)
    row = lax.broadcasted_iota(jnp.int32, (count, count), 0)
    column = lax.broadcasted_iota(jnp.int32, (count, count), 1)
    unit = (row == column).astype(jnp.float32).astype(jnp.bfloat16)
    cosine, sine = cosine_ref[...], sine_ref[...]
    scale = head_dim**-0.5 * math.log2(math.e)
    heads = width // head_dim
    for start in range(0, heads, 4):
        rows = jnp.concatenate(
            [
                jnp.concatenate(
                    [
                        turned(
                            queries_ref[:, h * head_dim : (h + 1) * head_dim].astype(jnp.float32),
                            cosine,
                            sine,
                        ).astype(jnp.bfloat16),
                        unit,
                    ],
                    axis=1,
                )
                for h in range(start, start + 4)
            ],
            axis=0,
        )
        scores = lax.dot_general(
            rows, keys, (((1,), (1,)), ((), ())), preferred_element_type=jnp.float32
        )
        top_score = jnp.max(scores, axis=1, keepdims=True)
        weights = jnp.exp2((scores - top_score) * scale)
        share = 1.0 / jnp.sum(weights, axis=1, keepdims=True)
        probs = (weights * share).astype(jnp.bfloat16)
        result = jnp.dot(probs, values, preferred_element_type=jnp.float32).astype(jnp.bfloat16)
        for h in range(4):
            out_ref[:, (start + h) * head_dim : (start + h + 1) * head_dim] = result[
                h * count : (h + 1) * count
            ]


def attend(offset, far, close, queries, first, cosine, sine):
    count, width = queries.shape
    return pl.pallas_call(
        attend_kernel,
        out_shape=jax.ShapeDtypeStruct((count, width), jnp.bfloat16),
        in_specs=[pl.BlockSpec(memory_space=pltpu.SMEM), *on_chip(6)],
        out_specs=on_chip(1)[0],
        scratch_shapes=[pltpu.VMEM((far.shape[1] + close.shape[1], close.shape[2]), jnp.bfloat16)] * 2,
        compiler_params=room(20),
        cost_estimate=pl.CostEstimate(
            flops=6 * count * width * 1152,
            bytes_accessed=4 * count * width + 2 * far.size + 2 * close.size,
            transcendentals=count * width * 9,
        ),
    )(offset, far, close, queries, first, cosine, sine)


def rotation_tables(places, head_dim):
    half_width = head_dim // 2
    freqs = jnp.exp(
        jnp.arange(half_width, dtype=jnp.float32) * (-2.0 * math.log(rope_base) / head_dim)
    )
    angles = places.astype(jnp.float32)[:, None] * freqs
    cosine = jnp.cos(angles)
    sine = jnp.sin(angles)
    return (
        jnp.concatenate([cosine, cosine], axis=1),
        jnp.concatenate([-sine, sine], axis=1),
    )


def shifted(value, axis, steps):
    count = lax.axis_size(axis)
    return lax.ppermute(value, axis, [(source, source + steps) for source in range(count - steps)])


def along_x(value, steps):
    pairs = []
    for x_lo in range(2):
        for x_hi in range(2):
            goal = (2 * x_hi + x_lo + steps) % 4
            pairs.append((2 * x_lo + x_hi, 2 * (goal % 2) + goal // 2))
    return lax.ppermute(value, ALONG_X, pairs)


def column_halves(rows, axes):
    half = rows.shape[1] // 2
    for_core = jnp.stack([rows[:, :half], rows[:, half:]])
    reach = lax.axis_size(axes[0])
    copies = jnp.broadcast_to(for_core, (reach, *for_core.shape)).reshape(-1, *for_core.shape[1:])
    return lax.all_to_all(copies, axes, split_axis=0, concat_axis=0, tiled=True)


def compute(tokens, queries, positions, grad, master, moment1, moment2, step):
    head_dim = master.shape[1] // 2
    local_count = tokens.shape[0]
    core = lax.axis_index(CORE)
    place = jnp.stack([core, 2 * lax.axis_index(X_HI) + lax.axis_index("x_lo")]).astype(jnp.int32)
    new_master, new_first, new_second = adam_update(grad, master, moment1, moment2, step)
    weight = new_master.astype(jnp.bfloat16)
    over_z = column_halves(weight, (ALONG_Z, CORE)).reshape(-1, head_dim)
    mine = split_columns(tokens)
    theirs = lax.ppermute(mine, CORE, [(0, 1), (1, 0)])
    places_both = lax.all_gather(positions, CORE, axis=0, tiled=True)
    places_other = jnp.where(core == 0, places_both[local_count:], places_both[:local_count])
    cosine, sine = rotation_tables(positions, head_dim)
    cosine_other, sine_other = rotation_tables(places_other, head_dim)
    is_keys = core == 0
    key_cosine = jnp.where(is_keys, jnp.concatenate([cosine, cosine_other]), 1.0)
    key_sine = jnp.where(is_keys, jnp.concatenate([sine, sine_other]), 0.0)
    first = jnp.broadcast_to(
        (jnp.arange(local_count, dtype=jnp.int32) - positions)[None, :], (8, local_count)
    )
    over_y = lax.all_gather(over_z, ALONG_Y, axis=0, tiled=True)
    half = over_y.shape[0] // 2
    tiles = (2 * local_count, head_dim)
    left = along_x(over_y, 1)
    right = along_x(over_y, 3)
    so_far = product(own_kernel, place, theirs, mine, tiles, jnp.float32, 1, over_y)
    across_low = along_x(left[:half], 1)
    across_high = along_x(right[half:], 3)
    so_far = product(beside_kernel, place, theirs, mine, tiles, jnp.float32, 2, so_far, left, right)
    half_kv = product(
        across_kernel, place, theirs, mine, tiles, jnp.bfloat16, 1,
        so_far, across_low, across_high, key_cosine, key_sine,
    )
    row_kv = lax.all_gather(half_kv, X_HI, axis=0, tiled=True)
    one_back = shifted(row_kv, CHIPS, 2)
    two_back = shifted(row_kv, CHIPS, 4)
    near_both = lax.all_gather(row_kv, CORE, axis=0)
    far_both = lax.all_gather(jnp.concatenate([two_back, one_back], axis=0), CORE, axis=0)
    offset = lax.axis_index(("x_hi", "core")) * local_count
    attention = attend(
        offset.astype(jnp.int32)[None], far_both, near_both, queries, first, cosine, sine
    )
    return (attention, new_master, new_first, new_second)


def solution(mesh):
    finer = Mesh(mesh.devices.reshape(2, 16, 8, 2, 2), EVERY)
    rows = P(EVERY, None)
    placed = (rows, rows, P(EVERY), rows, rows, rows, rows, P())
    return jax.shard_map(
        compute,
        mesh=finer,
        in_specs=placed,
        out_specs=(rows, rows, rows, rows),
        check_vma=False,
    )
```
